128 devices in a mesh: rep: 16 (over x, z), own: 8 (over y, core).
Axes of the slice: x: 4, y: 4, z: 4, core: 2. Of those that a mesh axis runs over, the one named last changes fastest.
Arguments:
- grads: bfloat16 [16, 8, 3, 768, 768], P('rep', 'own'), may hold values from -0.059814453 to 0.059814453
- weights: float32 [3, 768, 768], P(None, 'own'), may hold values from -0.21875 to 0.21875
- mom_first: float32 [3, 768, 768], P(None, 'own'), may hold values from -3 to 3
- mom_second: float32 [3, 768, 768], P(None, 'own'), may hold values from 0.003 to 0.03
- left_stat: float32 [8, 768, 768], P('own'), may hold values from -3 to 33, as said below
- right_stat: float32 [8, 768, 768], P('own'), may hold values from -3 to 33, as said below
- left_root: float32 [8, 768, 768], P('own'), may hold values from -1 to 4, as said below
- right_root: float32 [8, 768, 768], P('own'), may hold values from -1 to 4, as said below
- owners: int32 [3], replicated, may hold values from 0 to 7, as said below
Outputs:
- new_weights: float32 [3, 768, 768], P(None, 'own')
- new_mom_first: float32 [3, 768, 768], P(None, 'own')
- new_mom_second: float32 [3, 768, 768], P(None, 'own')
- new_left: float32 [8, 768, 768], P('own')
- new_right: float32 [8, 768, 768], P('own')
The draws below stay inside these ranges and needn't reach their ends.
Inputs may be any that keep to these rules, and one draw needn't show every extreme that they name: `owners`: the 3 entries are distinct, and one of them is always 8 - 1. `left_stat`: each slot is symmetric. `right_stat`: each slot is symmetric. `left_root`: each slot is symmetric. `right_root`: each slot is symmetric.
All inputs are finite; a program needn't handle non-finite values.
Results may differ from the reference program's by a relative error of at most 0.008.
Values may be sent and summed in bfloat16 or wider, within the bound.
A program may use at most 128 MiB of HBM per device.

```python
import math
import jax
import jax.numpy as jnp
from jax import lax

D = 768
ITEMS = 3
N_REP = 16
N_OWN = 8


def symmetric_part(key, scale):
    normal_part = jnp.clip(jax.random.normal(key, (N_OWN, D, D), jnp.float32), -6.0, 6.0)
    return (normal_part + jnp.swapaxes(normal_part, 1, 2)) * scale


def statistic(key):
    key_pair = jax.random.split(key)
    diagonal = jax.random.uniform(key_pair[1], (N_OWN, D), jnp.float32, 4.0, 16.0)
    off_part = symmetric_part(key_pair[0], 0.2)
    return off_part + diagonal[:, :, None] * jnp.eye(D, dtype=jnp.float32)


def inverse_root(key):
    key_pair = jax.random.split(key)
    low_end = jnp.log(0.3)
    off_part = symmetric_part(key_pair[0], 0.015)
    diagonal = jnp.exp(jax.random.uniform(key_pair[1], (N_OWN, D), jnp.float32, low_end, jnp.log(3.0)))
    return off_part + diagonal[:, :, None] * jnp.eye(D, dtype=jnp.float32)


def draw_left_stat(key, part):
    return statistic(jax.random.fold_in(key, 101))


def draw_right_stat(key, part):
    return statistic(jax.random.fold_in(key, 202))


def draw_left_root(key, part):
    return inverse_root(jax.random.fold_in(key, 303))


def draw_right_root(key, part):
    return inverse_root(jax.random.fold_in(key, 404))


def draw_mom_first(key, part):
    key_set = jax.random.split(jax.random.fold_in(key, 505), 3)
    line = jnp.arange(D, dtype=jnp.float32) / (D - 1)
    rising = 1.0 + 2.0 * line
    values = jnp.clip(jax.random.normal(key_set[0], (ITEMS, D, D), jnp.float32), -4.0, 4.0)
    rough = jnp.exp(jax.random.uniform(key_set[1], (ITEMS, D), jnp.float32, jnp.log(0.5), jnp.log(2.0)))
    column_scale = jnp.exp(jax.random.uniform(key_set[2], (ITEMS, D), jnp.float32, jnp.log(0.3), jnp.log(3.0)))
    row_scale = rising[None, :] * rough
    return 0.03 * values * row_scale[:, :, None] * column_scale[:, None, :]


def draw_owners(key, part):
    key_pair = jax.random.split(jax.random.fold_in(key, 606))
    others = jax.random.permutation(key_pair[0], N_OWN - 1)[:ITEMS - 1].astype(jnp.int32)
    listed = jnp.concatenate([others, jnp.full((1,), N_OWN - 1, jnp.int32)])
    order = jax.random.permutation(key_pair[1], ITEMS)
    return listed[order].astype(jnp.int32)


def level_of(own_key, extent, shards, smallest, high):
    gain, own = 1.0, jax.random.fold_in(own_key, 6)
    for dim, blocks in shards:
        heights = jnp.exp(jax.random.uniform(jax.random.fold_in(own, dim), (blocks,), jnp.float32, smallest / len(shards), high / len(shards)))
        gain = gain * jnp.repeat(heights, extent[dim] // blocks).reshape([-1 if axis == dim else 1 for axis in range(len(extent))])
    return gain


def bell_draw(stream_key, extent, scale, reach, cuts=(), held_as=jnp.bfloat16):
    values = jax.random.normal(stream_key, extent, jnp.float32) * scale
    if len(cuts) > 0:
        values = level_of(stream_key, extent, cuts, -0.22, 0.18) * values
    return jnp.clip(values, min=-reach, max=reach).astype(held_as)


def setup_inputs(seed: int = 0) -> dict:
    splits = jax.random.split(jax.random.key(seed), 10)
    grads = bell_draw(splits[0], (N_REP, N_OWN, ITEMS, D, D), 0.01, 0.059814453, ((0, 16), (1, 8)))
    weights = bell_draw(splits[1], (ITEMS, D, D), D ** -0.5, 0.21875, ((1, 8),), jnp.float32)
    mom_first = draw_mom_first(jax.random.fold_in(splits[9], 71), 0)
    mom_second = jnp.clip(jnp.exp(math.log(0.03) - 2.3025851 * jax.random.uniform(splits[3], (ITEMS, D, D), jnp.float32) ** level_of(splits[3], (ITEMS, D, D), ((1, 8),), -0.2, 0.2)), 0.003, 0.03)
    left_stat = draw_left_stat(jax.random.fold_in(splits[9], 71), 0)
    right_stat = draw_right_stat(jax.random.fold_in(splits[9], 71), 0)
    left_root = draw_left_root(jax.random.fold_in(splits[9], 71), 0)
    right_root = draw_right_root(jax.random.fold_in(splits[9], 71), 0)
    owners = draw_owners(jax.random.fold_in(splits[9], 71), 0)
    return dict(grads=grads, weights=weights, mom_first=mom_first, mom_second=mom_second, left_stat=left_stat, right_stat=right_stat, left_root=left_root, right_root=right_root, owners=owners)


first_decay = 0.9
second_decay = 0.95
adam_epsilon = 1e-08
graft_floor = 1e-06
learn_rate = 0.05

def accumulate(carry, piece):
    return (carry + piece.astype(jnp.float32), None)

def reference(grads, weights, mom_first, mom_second, left_stat, right_stat, left_root, right_root, owners):
    stacked = grads.reshape(N_REP * N_OWN, ITEMS, D, D)
    summed = lax.scan(accumulate, jnp.zeros((ITEMS, D, D), jnp.float32), stacked)[0]
    grad_sum = summed.astype(jnp.bfloat16)
    wide_grad = grad_sum.astype(jnp.float32)
    first_new = first_decay * mom_first + (1.0 - first_decay) * wide_grad
    second_new = second_decay * mom_second + (1.0 - second_decay) * wide_grad * wide_grad
    adam_step = first_new / (jnp.sqrt(second_new) + adam_epsilon)
    adam_mean = lax.optimization_barrier(jnp.mean(adam_step * adam_step, axis=(1, 2)))
    new_left = left_stat
    new_right = right_stat
    updated = []
    for position in range(ITEMS):
        owner = owners[position]
        grad_mat = grad_sum[position]
        left_old = lax.dynamic_index_in_dim(left_stat, owner, 0, keepdims=False)
        right_old = lax.dynamic_index_in_dim(right_stat, owner, 0, keepdims=False)
        left_inv = lax.dynamic_index_in_dim(left_root, owner, 0, keepdims=False)
        right_inv = lax.dynamic_index_in_dim(right_root, owner, 0, keepdims=False)
        left_new = left_old + jnp.einsum('ik,jk->ij', grad_mat, grad_mat, preferred_element_type=jnp.float32)
        right_new = right_old + jnp.einsum('ki,kj->ij', grad_mat, grad_mat, preferred_element_type=jnp.float32)
        new_left = lax.dynamic_update_index_in_dim(new_left, left_new, owner, 0)
        new_right = lax.dynamic_update_index_in_dim(new_right, right_new, owner, 0)
        half_product = jnp.dot(left_inv, wide_grad[position], precision=lax.Precision.HIGHEST)
        direction = jnp.dot(half_product, right_inv, precision=lax.Precision.HIGHEST)
        graft_scale = jnp.sqrt(adam_mean[position] / (jnp.mean(direction * direction) + graft_floor))
        updated.append(weights[position] - learn_rate * graft_scale * direction)
    new_weights = jnp.stack(updated)
    return (new_weights, first_new, second_new, new_left, new_right)
```

```python
import functools

import jax
import jax.numpy as jnp
from jax import lax
from jax.experimental import pallas as pl
from jax.experimental.pallas import tpu as pltpu
from jax.sharding import PartitionSpec as P

MESH = pl.DeviceIdType.MESH
F32 = jnp.float32
BF16 = jnp.bfloat16

first_decay = 0.9
second_decay = 0.95
adam_epsilon = 1e-08
graft_floor = 1e-06
learn_rate = 0.05

D = 768
ROWS = 96
HALF = 48
COLS = 384
SPLIT = 80
STEP = 16


def row_loop(rows, body):
    def run(i, carry):
        body(pl.ds(pl.multiple_of(i * STEP, STEP), STEP))
        return carry

    lax.fori_loop(0, rows // STEP, run, 0)


def kernel(
    grads, weights, mom_first, mom_second, left_stat, right_stat, left_root, right_root, owners,
    w_out, first_out, second_out, left_out, right_out,
    loc, pair, relay_up, relay_down, from_low, from_high, quads, part2, part3, g,
    root_wide, w_in, first_in, second_in,
    left_bf, left_pick, right_bf, h, piece, slots, picked,
    adam_mine, adam_all, square_mine, square_all,
    send_sem, recv_sem, local_sem,
):
    r = lax.axis_index("rep")
    o = lax.axis_index("own")
    x, z = r // 4, r % 4
    y, c = o // 2, o % 2
    other = 1 - c

    def at_x(d):
        return (((x + d) % 4) * 4 + z, o)

    def at_y(d):
        return (r, ((y + d) % 4) * 2 + c)

    def at_z(d):
        return (x * 4 + (z + d) % 4, o)

    partner = (r, y * 2 + other)
    ring = {"x": at_x, "y": at_y, "z": at_z}
    place = {"x": x, "y": y, "z": z}
    orders = ("yxz", "xzy", "zyx")

    count = [0]

    def send(src, dst, device):
        i = count[0]
        count[0] += 1
        copy = pltpu.make_async_remote_copy(
            src_ref=src, dst_ref=dst, send_sem=send_sem.at[i], recv_sem=recv_sem.at[i],
            device_id=device, device_id_type=MESH,
        )
        copy.start()
        started.append(copy)
        return copy

    started = []
    local_count = [0]

    def fetch(src, dst):
        i = local_count[0]
        local_count[0] += 1
        copy = pltpu.make_async_copy(src, dst, local_sem.at[i])
        copy.start()
        return copy

    def grad_rows(m, k, core):
        j = (place[orders[m][0]] + k) % 4
        start = pl.multiple_of((2 * j + core) * ROWS, ROWS)
        return grads.at[0, 0, m, pl.ds(start, ROWS), :]

    barrier = pltpu.get_barrier_semaphore()
    friends = [(r, (o + k) % 8) for k in range(1, 8)]
    friends += [at_x(k) for k in (1, 2, 3)] + [at_z(k) for k in (1, 2, 3)]
    for friend in friends:
        pl.semaphore_signal(barrier, inc=1, device_id=friend, device_id_type=MESH)

    own_half = {}
    for k in (2, 1, 3, 0):
        for m in range(3):
            own_half[m, k] = fetch(grad_rows(m, k, c), loc.at[m, k])
    pl.semaphore_wait(barrier, len(friends))

    pair_copy = {}
    for k in (2, 1, 3, 0):
        for m in range(3):
            pair_copy[m, k] = send(grad_rows(m, k, other), pair.at[m, k], partner)

    left_copy = fetch(left_root.at[0], root_wide.at[0])
    right_copy = fetch(right_root.at[0], root_wide.at[1])
    left_stat_copy = fetch(left_stat.at[0], left_out.at[0])
    right_stat_copy = fetch(right_stat.at[0], right_out.at[0])
    first_copy = fetch(mom_first, first_in)
    second_copy = fetch(mom_second, second_in)
    weight_copy = fetch(weights, w_in)

    def merge(dst, src, start, rows):
        def body(at):
            at = pl.ds(at.start + start, STEP) if start else at
            dst[at, :] = (dst[at, :].astype(F32) + src[at, :].astype(F32)).astype(BF16)

        row_loop(rows, body)

    def merge_pair(m, k):
        own_half[m, k].wait()
        pair_copy[m, k].wait_recv()
        merge(loc.at[m, k], pair.at[m, k], 0, ROWS)

    top, low = pl.ds(0, HALF), pl.ds(HALF, HALF)
    to_relay = {}
    for m in range(3):
        merge_pair(m, 2)
        ring1 = ring[orders[m][0]]
        to_relay[m, 1] = send(loc.at[m, 2, top], relay_up.at[m], ring1(1))
        to_relay[m, -1] = send(loc.at[m, 2, low], relay_down.at[m], ring1(-1))
    direct = {}
    for m in range(3):
        ring1 = ring[orders[m][0]]
        merge_pair(m, 1)
        direct[m, 1] = send(loc.at[m, 1, low], from_low.at[m, low], ring1(1))
        merge_pair(m, 3)
        direct[m, -1] = send(loc.at[m, 3, top], from_high.at[m, top], ring1(-1))
    relayed = {}
    for m in range(3):
        ring1 = ring[orders[m][0]]
        to_relay[m, 1].wait_recv()
        merge(loc.at[m, 1, top], relay_up.at[m], 0, HALF)
        relayed[m, 1] = send(loc.at[m, 1, top], from_low.at[m, top], ring1(1))
        to_relay[m, -1].wait_recv()
        merge(loc.at[m, 3, low], relay_down.at[m], 0, HALF)
        relayed[m, -1] = send(loc.at[m, 3, low], from_high.at[m, low], ring1(-1))
    for m in range(3):
        own_half[m, 0].wait()
        pair_copy[m, 0].wait_recv()

    left_copy.wait()
    right_copy.wait()

    def narrow(at):
        left_bf[at, :] = root_wide[0, at, :].astype(BF16)
        right_bf[at, :] = root_wide[1, at, :].astype(BF16)

    row_loop(D, narrow)
    for i in range(4):
        for parity, q in ((0, x), (1, z)):
            start = pl.multiple_of((2 * i + parity) * ROWS + HALF * (q // 2), STEP)
            left_pick[parity, pl.ds(HALF * i, HALF), :] = left_bf[pl.ds(start, HALF), :]

    second_ring = {}
    for m in range(3):
        for name in (1, -1):
            direct[m, name].wait_recv()
            relayed[m, name].wait_recv()
        for half in range(2):
            def total(at, m=m, half=half):
                rows = pl.ds(pl.multiple_of(at.start + half * HALF, STEP), STEP)
                value = loc[m, 0, rows, :].astype(F32) + pair[m, 0, rows, :].astype(F32)
                value += from_low[m, rows, :].astype(F32) + from_high[m, rows, :].astype(F32)
                value = value.astype(BF16)
                quads[m, 2 * half, at, :] = value[:, :COLS]
                quads[m, 2 * half + 1, at, :] = value[:, COLS:]

            row_loop(HALF, total)
        ring2, a2 = ring[orders[m][1]], place[orders[m][1]]
        for k in (2, 1, 3):
            second_ring[m, k] = send(quads.at[m, (a2 + k) % 4], part2.at[m, k - 1], ring2(k))

    third_ring = {}
    for m in range(3):
        a2, a3 = place[orders[m][1]], place[orders[m][2]]
        for k in (1, 3, 2):
            second_ring[m, k].wait_recv()

        def total(at, m=m, a2=a2, a3=a3):
            value = quads[m, a2, at, :].astype(F32) + part2[m, 0, at, :].astype(F32)
            value += part2[m, 1, at, :].astype(F32) + part2[m, 2, at, :].astype(F32)
            part3[m, a3, at, :] = value.astype(BF16)

        row_loop(HALF, total)
        ring3 = ring[orders[m][2]]
        for k in (2, 1, 3):
            third_ring[m, k] = send(part3.at[m, a3], part3.at[m, a3], ring3(k))

    def quadrant(m, j, q):
        start = pl.multiple_of((2 * j + c) * ROWS + HALF * (q // 2), STEP)
        return g.at[m, q % 2, pl.ds(start, HALF), :]

    gather2, gather1 = {}, {}

    def spread(m, k):
        ring1, a1, a2 = ring[orders[m][0]], place[orders[m][0]], place[orders[m][1]]
        here = quadrant(m, a1, (a2 - k) % 4)
        for d in (1, -1):
            gather1[m, k, d] = send(here, here, ring1(d))

    for m in range(3):
        a1, a2 = place[orders[m][0]], place[orders[m][1]]
        for k in (1, 3, 2):
            third_ring[m, k].wait_recv()
        here = quadrant(m, a1, a2)

        def total(at, m=m, here=here):
            value = part3[m, 0, at, :].astype(F32) + part3[m, 1, at, :].astype(F32)
            value += part3[m, 2, at, :].astype(F32) + part3[m, 3, at, :].astype(F32)
            here[at, :] = value.astype(BF16)

        row_loop(HALF, total)
        ring2 = ring[orders[m][1]]
        for k in (2, 1, 3):
            gather2[m, k] = send(here, here, ring2(k))
        spread(m, 0)
    for k in (1, 3, 2):
        for m in range(3):
            gather2[m, k].wait_recv()
            spread(m, k)

    shared = {}

    def share(m, k):
        j = (place[orders[m][0]] + k) % 4
        start = pl.multiple_of((2 * j + c) * ROWS, STEP)
        here = g.at[m, :, pl.ds(start, ROWS), :]
        shared[m, k] = send(here, here, partner)

    for m in range(3):
        share(m, 0)
    relay1 = {}
    for k, d in ((0, 1), (3, -1), (1, 1), (2, -1)):
        for m in range(3):
            ring1, a1, a2 = ring[orders[m][0]], place[orders[m][0]], place[orders[m][1]]
            gather1[m, k, d].wait_recv()
            there = quadrant(m, (a1 - d) % 4, (a2 - k) % 4)
            relay1[m, k] = send(there, there, ring1(d))
    for m in range(3):
        for k, d in ((2, 1), (3, 1), (0, -1), (1, -1)):
            gather1[m, k, d].wait_recv()
        share(m, 1)
        share(m, 3)
    for m in range(3):
        for k in range(4):
            relay1[m, k].wait_recv()
        share(m, 2)
    for m in range(3):
        for k in range(4):
            shared[m, k].wait_recv()

    item = jnp.where(owners[1] == o, 1, jnp.where(owners[2] == o, 2, 0))
    holding = jnp.where(owners[0] == o, 1, jnp.where(item > 0, 1, 0)).astype(F32)

    def half_rows(i, carry):
        at = pl.ds(pl.multiple_of(i * 192, 192), 192)
        value = jnp.dot(g[item, 0, at, :], right_bf[:COLS, :], preferred_element_type=F32)
        value += jnp.dot(g[item, 1, at, :], right_bf[COLS:, :], preferred_element_type=F32)
        value = value.astype(BF16)
        h[0, at, :] = value[:, :COLS]
        h[1, at, :] = value[:, COLS:]
        return carry

    lax.fori_loop(0, 4, half_rows, 0)
    for parity, q in ((0, x), (1, z)):
        value = jnp.dot(left_pick[parity], h[q % 2], preferred_element_type=F32).astype(BF16)
        for i in range(4):
            piece[2 * i + parity] = value[HALF * i : HALF * (i + 1), :]
    piece_copy = {}
    for k in range(1, 8):
        p = (o + k) % 8
        piece_copy[k] = send(piece.at[p], slots.at[o], (r, p))
    mine_copy = fetch(piece.at[o], slots.at[o])

    first_copy.wait()
    second_copy.wait()

    def fold(value):
        value = jnp.sum(value, axis=0, keepdims=True)
        return sum(value[:, 128 * i : 128 * (i + 1)] for i in range(value.shape[1] // 128))

    own_rows = pl.multiple_of(o * ROWS, STEP)
    for m in range(3):
        def moment(i, carry, m=m):
            at = pl.ds(pl.multiple_of(i * STEP, STEP), STEP)
            there = pl.ds(pl.multiple_of(own_rows + i * STEP, STEP), STEP)
            for half in range(2):
                cols = pl.ds(COLS * half, COLS)
                grad = g[m, half, there, :].astype(F32)
                first = first_decay * first_in[m, at, cols] + (1.0 - first_decay) * grad
                second = second_decay * second_in[m, at, cols] + (1.0 - second_decay) * grad * grad
                first_out[m, at, cols] = first
                second_out[m, at, cols] = second
                step = first / (jnp.sqrt(second) + adam_epsilon)
                carry = carry + fold(step * step)
            return carry

        total = lax.fori_loop(0, ROWS // STEP, moment, jnp.zeros((1, 128), F32))
        adam_mine[m] = jnp.broadcast_to(total, (8, 128))
    adam_copy = {}
    for k in range(1, 8):
        adam_copy[k] = send(adam_mine, adam_all.at[o], (r, (o + k) % 8))
    adam_local = fetch(adam_mine, adam_all.at[o])

    def square(i, carry):
        at = pl.ds(pl.multiple_of(i * 192, 192), 192)
        for half in range(2):
            value = jnp.dot(left_bf[at, :], h[half], preferred_element_type=F32)
            carry = carry + fold(value * value)
        return carry

    total = lax.fori_loop(0, 4, square, jnp.zeros((1, 128), F32))
    square_mine[...] = jnp.broadcast_to(total, (8, 128))
    square_copy = {}
    for k in range(1, 8):
        square_copy[k] = send(square_mine, square_all.at[o], (r, (o + k) % 8))
    square_local = fetch(square_mine, square_all.at[o])

    for k in range(1, 8):
        piece_copy[k].wait_recv()
    mine_copy.wait()
    a = x + c * (z - x)

    def near(d):
        return (other * (((x + d) % 4) * 4 + z) + c * (x * 4 + (z + d) % 4), o)

    for m in range(3):
        picked[a, pl.ds(HALF * m, HALF), :] = slots[owners[m]]
    upper, lower = pl.ds(0, SPLIT), pl.ds(SPLIT, 3 * HALF - SPLIT)
    update = {}
    for d, part in ((1, upper), (-1, lower), (1, lower), (-1, upper)):
        here = picked.at[a, part]
        update[d, part is upper] = send(here, here, near(d))

    left_stat_copy.wait()

    def left_rows(i, carry):
        at = pl.ds(pl.multiple_of(i * 192, 192), 192)
        dims = (((1,), (1,)), ((), ()))
        value = lax.dot_general(g[item, 0, at, :], g[item, 0], dims, preferred_element_type=F32)
        value += lax.dot_general(g[item, 1, at, :], g[item, 1], dims, preferred_element_type=F32)
        left_out[0, at, :] = left_out[0, at, :] + holding * value
        return carry

    lax.fori_loop(0, 4, left_rows, 0)

    onward = {}
    for d, part in ((1, upper), (-1, lower)):
        update[d, part is upper].wait_recv()
        there = picked.at[(a - d) % 4, part]
        onward[d] = send(there, there, near(d))

    right_stat_copy.wait()
    dims = (((0,), (0,)), ((), ()))
    for i in range(2):
        for j in range(2):
            value = lax.dot_general(g[item, i], g[item, j], dims, preferred_element_type=F32)
            rows, cols = pl.ds(COLS * i, COLS), pl.ds(COLS * j, COLS)
            right_out[0, rows, cols] = right_out[0, rows, cols] + holding * value

    weight_copy.wait()
    for k in range(1, 8):
        adam_copy[k].wait_recv()
        square_copy[k].wait_recv()
    adam_local.wait()
    square_local.wait()
    rates = []
    for m in range(3):
        adam_total = adam_all[0, m, 0:1, :]
        for p in range(1, 8):
            adam_total = adam_total + adam_all[p, m, 0:1, :]
        adam_mean = jnp.sum(adam_total, axis=1, keepdims=True) / (D * D)
        squares = square_all[owners[m]][0:1, :]
        mean = jnp.sum(squares, axis=1, keepdims=True) / (D * D)
        rates.append(learn_rate * jnp.sqrt(adam_mean / (mean + graft_floor)))

    update[1, False].wait_recv()
    update[-1, True].wait_recv()
    onward[1].wait_recv()
    onward[-1].wait_recv()
    for m in range(3):
        for q in range(4):
            rows, cols = pl.ds(HALF * (q // 2), HALF), pl.ds(COLS * (q % 2), COLS)
            value = picked[q, pl.ds(HALF * m, HALF), :].astype(F32)
            w_out[m, rows, cols] = w_in[m, rows, cols] - rates[m] * value

    for copy in started:
        copy.wait_send()


def on_device(
    grads, weights, mom_first, mom_second, left_stat, right_stat, left_root, right_root, owners
):
    rows = jax.ShapeDtypeStruct((3, ROWS, D), F32)
    matrix = jax.ShapeDtypeStruct((1, D, D), F32)
    anywhere = pl.BlockSpec(memory_space=pl.ANY)
    vmem = pl.BlockSpec(memory_space=pltpu.VMEM)
    return pl.pallas_call(
        kernel,
        out_shape=(rows, rows, rows, matrix, matrix),
        in_specs=[anywhere] * 8 + [pl.BlockSpec(memory_space=pltpu.SMEM)],
        out_specs=(vmem,) * 5,
        scratch_shapes=[
            pltpu.VMEM((3, 4, ROWS, D), BF16),
            pltpu.VMEM((3, 4, ROWS, D), BF16),
            pltpu.VMEM((3, HALF, D), BF16),
            pltpu.VMEM((3, HALF, D), BF16),
            pltpu.VMEM((3, ROWS, D), BF16),
            pltpu.VMEM((3, ROWS, D), BF16),
            pltpu.VMEM((3, 4, HALF, COLS), BF16),
            pltpu.VMEM((3, 3, HALF, COLS), BF16),
            pltpu.VMEM((3, 4, HALF, COLS), BF16),
            pltpu.VMEM((3, 2, D, COLS), BF16),
            pltpu.VMEM((2, D, D), F32),
            pltpu.VMEM((3, ROWS, D), F32),
            pltpu.VMEM((3, ROWS, D), F32),
            pltpu.VMEM((3, ROWS, D), F32),
            pltpu.VMEM((D, D), BF16),
            pltpu.VMEM((2, 4 * HALF, D), BF16),
            pltpu.VMEM((D, D), BF16),
            pltpu.VMEM((2, D, COLS), BF16),
            pltpu.VMEM((8, HALF, COLS), BF16),
            pltpu.VMEM((8, HALF, COLS), BF16),
            pltpu.VMEM((4, 3 * HALF, COLS), BF16),
            pltpu.VMEM((3, 8, 128), F32),
            pltpu.VMEM((8, 3, 8, 128), F32),
            pltpu.VMEM((8, 128), F32),
            pltpu.VMEM((8, 8, 128), F32),
            pltpu.SemaphoreType.DMA((160,)),
            pltpu.SemaphoreType.DMA((160,)),
            pltpu.SemaphoreType.DMA((24,)),
        ],
        compiler_params=pltpu.CompilerParams(
            collective_id=0, has_side_effects=True, vmem_limit_bytes=56 * 1024 * 1024
        ),
    )(grads, weights, mom_first, mom_second, left_stat, right_stat, left_root, right_root, owners)


def solution(mesh):
    placed = (
        P("rep", "own", None, None, None),
        P(None, "own", None),
        P(None, "own", None),
        P(None, "own", None),
        P("own", None, None),
        P("own", None, None),
        P("own", None, None),
        P("own", None, None),
        P(),
    )
    return jax.shard_map(
        on_device,
        mesh=mesh,
        in_specs=placed,
        out_specs=(
            P(None, "own", None),
            P(None, "own", None),
            P(None, "own", None),
            P("own", None, None),
            P("own", None, None),
        ),
        check_vma=False,
    )
```

```python
import functools

import jax
import jax.numpy as jnp
from jax import lax
from jax.experimental import pallas as pl
from jax.experimental.pallas import tpu as pltpu
from jax.sharding import PartitionSpec as P

MESH = pl.DeviceIdType.MESH
F32 = jnp.float32
BF16 = jnp.bfloat16

first_decay = 0.9
second_decay = 0.95
adam_epsilon = 1e-08
graft_floor = 1e-06
learn_rate = 0.05

D = 768
ROWS = 96
HALF = 48
COLS = 384
SPLIT = 80
STEP = 16


def row_loop(rows, body):
    def run(i, carry):
        body(pl.ds(pl.multiple_of(i * STEP, STEP), STEP))
        return carry

    lax.fori_loop(0, rows // STEP, run, 0)


def kernel(
    grads, weights, mom_first, mom_second, left_stat, right_stat, left_root, right_root, owners_in,
    w_out, first_out, second_out, left_out, right_out,
    loc, pair, relay_up, relay_down, from_low, from_high, quads, part2, part3, g,
    root_wide, w_in, first_in, second_in,
    left_bf, left_pick, left_rest, right_bf, h, h_rest, piece, slots, picked,
    adam_mine, adam_all, square_mine, square_all,
    owners, send_sem, recv_sem, local_sem,
):
    r = lax.axis_index("rep")
    o = lax.axis_index("own")
    x, z = r // 4, r % 4
    y, c = o // 2, o % 2
    other = 1 - c

    def at_x(d):
        return (((x + d) % 4) * 4 + z, o)

    def at_y(d):
        return (r, ((y + d) % 4) * 2 + c)

    def at_z(d):
        return (x * 4 + (z + d) % 4, o)

    partner = (r, y * 2 + other)
    ring = {"x": at_x, "y": at_y, "z": at_z}
    place = {"x": x, "y": y, "z": z}
    orders = ("yxz", "xzy", "zyx")

    count = [0]

    def send(src, dst, device):
        i = count[0]
        count[0] += 1
        copy = pltpu.make_async_remote_copy(
            src_ref=src, dst_ref=dst, send_sem=send_sem.at[i], recv_sem=recv_sem.at[i],
            device_id=device, device_id_type=MESH,
        )
        copy.start()
        started.append(copy)
        return copy

    started = []
    local_count = [0]

    def fetch(src, dst):
        i = local_count[0]
        local_count[0] += 1
        copy = pltpu.make_async_copy(src, dst, local_sem.at[i])
        copy.start()
        return copy

    def grad_rows(m, k, core):
        j = (place[orders[m][0]] + k) % 4
        start = pl.multiple_of((2 * j + core) * ROWS, ROWS)
        return grads.at[0, 0, m, pl.ds(start, ROWS), :]

    barrier = pltpu.get_barrier_semaphore()
    friends = [(r, (o + k) % 8) for k in range(1, 8)]
    friends += [at_x(k) for k in (1, 2, 3)] + [at_z(k) for k in (1, 2, 3)]
    for friend in friends:
        pl.semaphore_signal(barrier, inc=1, device_id=friend, device_id_type=MESH)

    own_half = {}
    for k in (2, 1, 3, 0):
        for m in range(3):
            own_half[m, k] = fetch(grad_rows(m, k, c), loc.at[m, k])
    pl.semaphore_wait(barrier, len(friends))

    pair_copy = {}
    for k in (2, 1, 3, 0):
        for m in range(3):
            pair_copy[m, k] = send(grad_rows(m, k, other), pair.at[m, k], partner)

    owner_copy = fetch(owners_in, owners)
    left_copy = fetch(left_root.at[0], root_wide.at[0])
    right_copy = fetch(right_root.at[0], root_wide.at[1])
    left_stat_copy = fetch(left_stat.at[0], left_out.at[0])
    right_stat_copy = fetch(right_stat.at[0], right_out.at[0])
    first_copy = fetch(mom_first, first_in)
    second_copy = fetch(mom_second, second_in)
    weight_copy = fetch(weights, w_in)

    def merge(dst, src, start, rows):
        def body(at):
            at = pl.ds(at.start + start, STEP) if start else at
            dst[at, :] = (dst[at, :].astype(F32) + src[at, :].astype(F32)).astype(BF16)

        row_loop(rows, body)

    def merge_pair(m, k):
        own_half[m, k].wait()
        pair_copy[m, k].wait_recv()
        merge(loc.at[m, k], pair.at[m, k], 0, ROWS)

    top, low = pl.ds(0, HALF), pl.ds(HALF, HALF)
    to_relay = {}
    for m in range(3):
        merge_pair(m, 2)
        ring1 = ring[orders[m][0]]
        to_relay[m, 1] = send(loc.at[m, 2, top], relay_up.at[m], ring1(1))
        to_relay[m, -1] = send(loc.at[m, 2, low], relay_down.at[m], ring1(-1))
    direct = {}
    for m in range(3):
        ring1 = ring[orders[m][0]]
        merge_pair(m, 1)
        direct[m, 1] = send(loc.at[m, 1, low], from_low.at[m, low], ring1(1))
        merge_pair(m, 3)
        direct[m, -1] = send(loc.at[m, 3, top], from_high.at[m, top], ring1(-1))
    relayed = {}
    for m in range(3):
        ring1 = ring[orders[m][0]]
        to_relay[m, 1].wait_recv()
        merge(loc.at[m, 1, top], relay_up.at[m], 0, HALF)
        relayed[m, 1] = send(loc.at[m, 1, top], from_low.at[m, top], ring1(1))
        to_relay[m, -1].wait_recv()
        merge(loc.at[m, 3, low], relay_down.at[m], 0, HALF)
        relayed[m, -1] = send(loc.at[m, 3, low], from_high.at[m, low], ring1(-1))
    for m in range(3):
        own_half[m, 0].wait()
        pair_copy[m, 0].wait_recv()

    left_copy.wait()
    right_copy.wait()

    def narrow(at):
        left_bf[at, :] = root_wide[0, at, :].astype(BF16)
        right_bf[at, :] = root_wide[1, at, :].astype(BF16)

    row_loop(D, narrow)
    for parity, q in ((0, x), (1, z)):
        for i in range(4):
            start = pl.multiple_of((2 * i + parity) * ROWS + HALF * (q // 2), STEP)
            wide = root_wide[0, pl.ds(start, HALF), :]
            high = wide.astype(BF16)
            left_pick[parity, pl.ds(HALF * i, HALF), :] = high
            left_rest[parity, pl.ds(HALF * i, HALF), :] = (wide - high.astype(F32)).astype(BF16)

    second_ring = {}
    for m in range(3):
        for name in (1, -1):
            direct[m, name].wait_recv()
            relayed[m, name].wait_recv()
        for half in range(2):
            def total(at, m=m, half=half):
                rows = pl.ds(pl.multiple_of(at.start + half * HALF, STEP), STEP)
                value = loc[m, 0, rows, :].astype(F32) + pair[m, 0, rows, :].astype(F32)
                value += from_low[m, rows, :].astype(F32) + from_high[m, rows, :].astype(F32)
                value = value.astype(BF16)
                quads[m, 2 * half, at, :] = value[:, :COLS]
                quads[m, 2 * half + 1, at, :] = value[:, COLS:]

            row_loop(HALF, total)
        ring2, a2 = ring[orders[m][1]], place[orders[m][1]]
        for k in (2, 1, 3):
            second_ring[m, k] = send(quads.at[m, (a2 + k) % 4], part2.at[m, k - 1], ring2(k))

    third_ring = {}
    for m in range(3):
        a2, a3 = place[orders[m][1]], place[orders[m][2]]
        for k in (1, 3, 2):
            second_ring[m, k].wait_recv()

        def total(at, m=m, a2=a2, a3=a3):
            value = quads[m, a2, at, :].astype(F32) + part2[m, 0, at, :].astype(F32)
            value += part2[m, 1, at, :].astype(F32) + part2[m, 2, at, :].astype(F32)
            part3[m, a3, at, :] = value.astype(BF16)

        row_loop(HALF, total)
        ring3 = ring[orders[m][2]]
        for k in (2, 1, 3):
            third_ring[m, k] = send(part3.at[m, a3], part3.at[m, a3], ring3(k))

    def quadrant(m, j, q):
        start = pl.multiple_of((2 * j + c) * ROWS + HALF * (q // 2), STEP)
        return g.at[m, q % 2, pl.ds(start, HALF), :]

    gather2, gather1 = {}, {}

    def spread(m, k):
        ring1, a1, a2 = ring[orders[m][0]], place[orders[m][0]], place[orders[m][1]]
        here = quadrant(m, a1, (a2 - k) % 4)
        for d in (1, -1):
            gather1[m, k, d] = send(here, here, ring1(d))

    for m in range(3):
        a1, a2 = place[orders[m][0]], place[orders[m][1]]
        for k in (1, 3, 2):
            third_ring[m, k].wait_recv()
        here = quadrant(m, a1, a2)

        def total(at, m=m, here=here):
            value = part3[m, 0, at, :].astype(F32) + part3[m, 1, at, :].astype(F32)
            value += part3[m, 2, at, :].astype(F32) + part3[m, 3, at, :].astype(F32)
            here[at, :] = value.astype(BF16)

        row_loop(HALF, total)
        ring2 = ring[orders[m][1]]
        for k in (2, 1, 3):
            gather2[m, k] = send(here, here, ring2(k))
        spread(m, 0)
    for k in (1, 3, 2):
        for m in range(3):
            gather2[m, k].wait_recv()
            spread(m, k)

    shared = {}

    def share(m, k):
        j = (place[orders[m][0]] + k) % 4
        start = pl.multiple_of((2 * j + c) * ROWS, STEP)
        here = g.at[m, :, pl.ds(start, ROWS), :]
        shared[m, k] = send(here, here, partner)

    for m in range(3):
        share(m, 0)
    relay1 = {}
    for k, d in ((0, 1), (3, -1), (1, 1), (2, -1)):
        for m in range(3):
            ring1, a1, a2 = ring[orders[m][0]], place[orders[m][0]], place[orders[m][1]]
            gather1[m, k, d].wait_recv()
            there = quadrant(m, (a1 - d) % 4, (a2 - k) % 4)
            relay1[m, k] = send(there, there, ring1(d))
    for m in range(3):
        for k, d in ((2, 1), (3, 1), (0, -1), (1, -1)):
            gather1[m, k, d].wait_recv()
        share(m, 1)
        share(m, 3)
    for m in range(3):
        for k in range(4):
            relay1[m, k].wait_recv()
        share(m, 2)
    for m in range(3):
        for k in range(4):
            shared[m, k].wait_recv()

    owner_copy.wait()
    item = jnp.where(owners[1] == o, 1, jnp.where(owners[2] == o, 2, 0))
    holding = jnp.where(owners[0] == o, 1, jnp.where(item > 0, 1, 0)).astype(F32)

    def half_rows(i, carry):
        at = pl.ds(pl.multiple_of(i * 192, 192), 192)
        value = jnp.dot(g[item, 0, at, :], right_bf[:COLS, :], preferred_element_type=F32)
        value += jnp.dot(g[item, 1, at, :], right_bf[COLS:, :], preferred_element_type=F32)
        high = value.astype(BF16)
        rest = (value - high.astype(F32)).astype(BF16)
        h[0, at, :] = high[:, :COLS]
        h[1, at, :] = high[:, COLS:]
        h_rest[0, at, :] = rest[:, :COLS]
        h_rest[1, at, :] = rest[:, COLS:]
        return carry

    lax.fori_loop(0, 4, half_rows, 0)
    for parity, q in ((0, x), (1, z)):
        value = jnp.dot(left_pick[parity], h[q % 2], preferred_element_type=F32)
        value += jnp.dot(left_rest[parity], h[q % 2], preferred_element_type=F32)
        value += jnp.dot(left_pick[parity], h_rest[q % 2], preferred_element_type=F32)
        value = value.astype(BF16)
        for i in range(4):
            piece[2 * i + parity] = value[HALF * i : HALF * (i + 1), :]
    piece_copy = {}
    for k in range(1, 8):
        p = (o + k) % 8
        piece_copy[k] = send(piece.at[p], slots.at[o], (r, p))
    mine_copy = fetch(piece.at[o], slots.at[o])

    first_copy.wait()
    second_copy.wait()

    def fold(value):
        value = jnp.sum(value, axis=0, keepdims=True)
        return sum(value[:, 128 * i : 128 * (i + 1)] for i in range(value.shape[1] // 128))

    own_rows = pl.multiple_of(o * ROWS, STEP)
    for m in range(3):
        def moment(i, carry, m=m):
            at = pl.ds(pl.multiple_of(i * STEP, STEP), STEP)
            there = pl.ds(pl.multiple_of(own_rows + i * STEP, STEP), STEP)
            for half in range(2):
                cols = pl.ds(COLS * half, COLS)
                grad = g[m, half, there, :].astype(F32)
                first = first_decay * first_in[m, at, cols] + (1.0 - first_decay) * grad
                second = second_decay * second_in[m, at, cols] + (1.0 - second_decay) * grad * grad
                first_out[m, at, cols] = first
                second_out[m, at, cols] = second
                step = first / (jnp.sqrt(second) + adam_epsilon)
                carry = carry + fold(step * step)
            return carry

        total = lax.fori_loop(0, ROWS // STEP, moment, jnp.zeros((1, 128), F32))
        adam_mine[m] = jnp.broadcast_to(total, (8, 128))
    adam_copy = {}
    for k in range(1, 8):
        adam_copy[k] = send(adam_mine, adam_all.at[o], (r, (o + k) % 8))
    adam_local = fetch(adam_mine, adam_all.at[o])

    def square(i, carry):
        at = pl.ds(pl.multiple_of(i * 192, 192), 192)
        for half in range(2):
            value = jnp.dot(left_bf[at, :], h[half], preferred_element_type=F32)
            carry = carry + fold(value * value)
        return carry

    total = lax.fori_loop(0, 4, square, jnp.zeros((1, 128), F32))
    square_mine[...] = jnp.broadcast_to(total, (8, 128))
    square_copy = {}
    for k in range(1, 8):
        square_copy[k] = send(square_mine, square_all.at[o], (r, (o + k) % 8))
    square_local = fetch(square_mine, square_all.at[o])

    for k in range(1, 8):
        piece_copy[k].wait_recv()
    mine_copy.wait()
    a = x + c * (z - x)

    def near(d):
        return (other * (((x + d) % 4) * 4 + z) + c * (x * 4 + (z + d) % 4), o)

    for m in range(3):
        picked[a, pl.ds(HALF * m, HALF), :] = slots[owners[m]]
    upper, lower = pl.ds(0, SPLIT), pl.ds(SPLIT, 3 * HALF - SPLIT)
    update = {}
    for d, part in ((1, upper), (-1, lower), (1, lower), (-1, upper)):
        here = picked.at[a, part]
        update[d, part is upper] = send(here, here, near(d))

    left_stat_copy.wait()

    def left_rows(i, carry):
        at = pl.ds(pl.multiple_of(i * 192, 192), 192)
        dims = (((1,), (1,)), ((), ()))
        value = lax.dot_general(g[item, 0, at, :], g[item, 0], dims, preferred_element_type=F32)
        value += lax.dot_general(g[item, 1, at, :], g[item, 1], dims, preferred_element_type=F32)
        left_out[0, at, :] = left_out[0, at, :] + holding * value
        return carry

    lax.fori_loop(0, 4, left_rows, 0)

    onward = {}
    for d, part in ((1, upper), (-1, lower)):
        update[d, part is upper].wait_recv()
        there = picked.at[(a - d) % 4, part]
        onward[d] = send(there, there, near(d))

    right_stat_copy.wait()
    dims = (((0,), (0,)), ((), ()))
    for i in range(2):
        for j in range(2):
            value = lax.dot_general(g[item, i], g[item, j], dims, preferred_element_type=F32)
            rows, cols = pl.ds(COLS * i, COLS), pl.ds(COLS * j, COLS)
            right_out[0, rows, cols] = right_out[0, rows, cols] + holding * value

    weight_copy.wait()
    for k in range(1, 8):
        adam_copy[k].wait_recv()
        square_copy[k].wait_recv()
    adam_local.wait()
    square_local.wait()
    rates = []
    for m in range(3):
        adam_total = adam_all[0, m, 0:1, :]
        for p in range(1, 8):
            adam_total = adam_total + adam_all[p, m, 0:1, :]
        adam_mean = jnp.sum(adam_total, axis=1, keepdims=True) / (D * D)
        squares = square_all[owners[m]][0:1, :]
        mean = jnp.sum(squares, axis=1, keepdims=True) / (D * D)
        rates.append(learn_rate * jnp.sqrt(adam_mean / (mean + graft_floor)))

    update[1, False].wait_recv()
    update[-1, True].wait_recv()
    onward[1].wait_recv()
    onward[-1].wait_recv()
    for m in range(3):
        for q in range(4):
            rows, cols = pl.ds(HALF * (q // 2), HALF), pl.ds(COLS * (q % 2), COLS)
            value = picked[q, pl.ds(HALF * m, HALF), :].astype(F32)
            w_out[m, rows, cols] = w_in[m, rows, cols] - rates[m] * value

    for copy in started:
        copy.wait_send()


def store(*refs):
    copies = [pltpu.make_async_copy(refs[i], refs[5 + i], refs[10].at[i]) for i in range(5)]
    for copy in copies:
        copy.start()
    for copy in copies:
        copy.wait()


def on_device(
    grads, weights, mom_first, mom_second, left_stat, right_stat, left_root, right_root, owners
):
    rows = jax.ShapeDtypeStruct((3, ROWS, D), F32)
    matrix = jax.ShapeDtypeStruct((1, D, D), F32)
    hbm = pl.BlockSpec(memory_space=pltpu.HBM)
    vmem = pl.BlockSpec(memory_space=pltpu.VMEM)
    outs = pl.pallas_call(
        kernel,
        out_shape=(pltpu.VMEM((3, ROWS, D), F32),) * 3 + (pltpu.VMEM((1, D, D), F32),) * 2,
        in_specs=[hbm] * 9,
        out_specs=(vmem,) * 5,
        scratch_shapes=[
            pltpu.VMEM((3, 4, ROWS, D), BF16),
            pltpu.VMEM((3, 4, ROWS, D), BF16),
            pltpu.VMEM((3, HALF, D), BF16),
            pltpu.VMEM((3, HALF, D), BF16),
            pltpu.VMEM((3, ROWS, D), BF16),
            pltpu.VMEM((3, ROWS, D), BF16),
            pltpu.VMEM((3, 4, HALF, COLS), BF16),
            pltpu.VMEM((3, 3, HALF, COLS), BF16),
            pltpu.VMEM((3, 4, HALF, COLS), BF16),
            pltpu.VMEM((3, 2, D, COLS), BF16),
            pltpu.VMEM((2, D, D), F32),
            pltpu.VMEM((3, ROWS, D), F32),
            pltpu.VMEM((3, ROWS, D), F32),
            pltpu.VMEM((3, ROWS, D), F32),
            pltpu.VMEM((D, D), BF16),
            pltpu.VMEM((2, 4 * HALF, D), BF16),
            pltpu.VMEM((2, 4 * HALF, D), BF16),
            pltpu.VMEM((D, D), BF16),
            pltpu.VMEM((2, D, COLS), BF16),
            pltpu.VMEM((2, D, COLS), BF16),
            pltpu.VMEM((8, HALF, COLS), BF16),
            pltpu.VMEM((8, HALF, COLS), BF16),
            pltpu.VMEM((4, 3 * HALF, COLS), BF16),
            pltpu.VMEM((3, 8, 128), F32),
            pltpu.VMEM((8, 3, 8, 128), F32),
            pltpu.VMEM((8, 128), F32),
            pltpu.VMEM((8, 8, 128), F32),
            pltpu.SMEM((3,), jnp.int32),
            pltpu.SemaphoreType.DMA((160,)),
            pltpu.SemaphoreType.DMA((160,)),
            pltpu.SemaphoreType.DMA((24,)),
        ],
        compiler_params=pltpu.CompilerParams(
            collective_id=0, has_side_effects=True, vmem_limit_bytes=50 * 1024 * 1024
        ),
    )(grads, weights, mom_first, mom_second, left_stat, right_stat, left_root, right_root, owners)
    return pl.pallas_call(
        store,
        out_shape=(rows, rows, rows, matrix, matrix),
        in_specs=[vmem] * 5,
        out_specs=(pl.BlockSpec(memory_space=pl.ANY),) * 5,
        scratch_shapes=[pltpu.SemaphoreType.DMA((5,))],
        compiler_params=pltpu.CompilerParams(vmem_limit_bytes=1024 * 1024),
    )(*outs)


def solution(mesh):
    placed = (
        P("rep", "own", None, None, None),
        P(None, "own", None),
        P(None, "own", None),
        P(None, "own", None),
        P("own", None, None),
        P("own", None, None),
        P("own", None, None),
        P("own", None, None),
        P(),
    )
    return jax.shard_map(
        on_device,
        mesh=mesh,
        in_specs=placed,
        out_specs=(
            P(None, "own", None),
            P(None, "own", None),
            P(None, "own", None),
            P("own", None, None),
            P("own", None, None),
        ),
        check_vma=False,
    )
```
